32 devices in a mesh: dp: 8 (over z, x), segment: 4 (over y, core).
Axes of the slice: x: 2, y: 2, z: 4, core: 2. Of those that a mesh axis runs over, the one named last changes fastest.
Arguments:
- features: bfloat16 [1536, 640], P('dp'), may hold values from -6 to 6
- timesteps: int32 [24], P('dp'), may hold values from 0 to 999
- text_ids: int32 [24, 64], replicated, may hold values from 0 to 16383
- text_table: bfloat16 [16384, 640], P(('dp', 'segment')), may hold values from -12 to 12
- in_weights: bfloat16 [4, 640, 640], P('segment'), may hold values from -0.25 to 0.25
- out_weights: bfloat16 [4, 640, 640], P('segment'), may hold values from -0.25 to 0.25
- skip_weights: bfloat16 [4, 640, 640], P('segment'), may hold values from -0.25 to 0.25
- cotangent: bfloat16 [1536, 640], P('dp'), may hold values from -0.15234375 to 0.15234375
Outputs:
- in_grads: float32 [4, 640, 640], P('segment', 'dp')
- out_grads: float32 [4, 640, 640], P('segment', 'dp')
- skip_grads: float32 [4, 640, 640], P('segment', 'dp')
The draws below stay inside these ranges and needn't reach their ends.
All inputs are finite; a program needn't handle non-finite values.
Results may differ from the reference program's by a relative error of at most 0.033.
Values may be sent and summed in bfloat16 or wider, within the bound.
No kernel may reach another device: no remote copies, remote signals or barrier semaphores. Data moves between devices by JAX's collectives and lax.ppermute only.
A program may use at most 64 MiB of HBM per device.

```python
import math
import jax
import jax.numpy as jnp
import numpy as np
from jax import lax

C = 640
GROUPS = 32
MB = 3
TEXT_LEN = 64
VOCAB = 16384
ROWS = 64
BATCH = 24
N_DP = 8
N_SEGMENT = 4


def touch_ends(array, own_key, least, high):
    longest = array.shape.index(max(array.shape))
    spots = []
    for shift in (0, 1):
        where = [jax.random.randint(jax.random.fold_in(own_key, axis), (), 0, length) for axis, length in enumerate(array.shape)]
        where[longest] = (where[longest] + shift) % array.shape[longest]
        spots.append(tuple(where))
    return array.at[spots[0]].set(least).at[spots[1]].set(high)


def levels(rng, dims, cuts, low, largest):
    gain, own = 1.0, jax.random.fold_in(rng, 6)
    for dim, shards_of in cuts:
        draws = jnp.exp(jax.random.uniform(jax.random.fold_in(own, dim), (shards_of,), jnp.float32, low / len(cuts), largest / len(cuts)))
        gain = gain * jnp.repeat(draws, dims[dim] // shards_of).reshape([-1 if axis == dim else 1 for axis in range(len(dims))])
    return gain


def rank_bounds(number_of, lean):
    portions = [(1 << 20) // math.isqrt(standing ** lean) + 1 for standing in range(1, number_of + 1)]
    scale = 1 + sum(portions) // (1 << 30)
    return np.cumsum(np.array([max(1, weight // scale) for weight in portions]))


def ranked(key, dims, count, slope):
    listing = rank_bounds(count, slope)
    pick = jax.random.randint(jax.random.fold_in(key, 1), dims, 0, int(listing[count - 1]))
    rank = jnp.searchsorted(jnp.asarray(listing, jnp.int32), pick, side="right")
    return jax.random.permutation(jax.random.fold_in(key, 2), count)[rank].astype(jnp.int32)


def noise(rng, extent, deviation, limit, shards=(), held_as=jnp.bfloat16):
    entries = jax.random.normal(rng, extent, jnp.float32) * deviation
    if len(shards) > 0:
        entries = levels(rng, extent, shards, -0.22, 0.18) * entries
    return jnp.clip(entries, min=-limit, max=limit).astype(held_as)


def setup_inputs(seed: int = 0) -> dict:
    keys = jax.random.split(jax.random.key(seed), 9)
    return {
        "features": noise(keys[0], (BATCH * ROWS, C), 1.0, 6.0, ((0, 8),)),
        "timesteps": touch_ends(jax.random.randint(keys[1], (BATCH,), 0, 1000), jax.random.fold_in(keys[1], 1), 0, 999).astype(jnp.int32),
        "text_ids": touch_ends(ranked(keys[2], (BATCH, TEXT_LEN), VOCAB, 2), jax.random.fold_in(keys[2], 3), 0, VOCAB - 1).astype(jnp.int32),
        "text_table": noise(keys[3], (VOCAB, C), 2.0, 12.0, ((0, 32),)),
        "in_weights": noise(keys[4], (N_SEGMENT, C, C), C ** -0.5, 0.25, ((0, 4),)),
        "out_weights": noise(keys[5], (N_SEGMENT, C, C), C ** -0.5, 0.25, ((0, 4),)),
        "skip_weights": noise(keys[6], (N_SEGMENT, C, C), C ** -0.5, 0.25, ((0, 4),)),
        "cotangent": noise(keys[7], (BATCH * ROWS, C), ((MB * N_DP * ROWS) ** -0.5), 0.15234375, ((0, 8),)),
    }


EPSILON = 1e-05

def grouped(vector):
    lead = vector.shape[:-1]
    split = vector.reshape(lead + (GROUPS, vector.shape[-1] // GROUPS))
    total = lax.optimization_barrier(jnp.sum(split, axis=-1, keepdims=True))
    return jnp.broadcast_to(total, split.shape).reshape(vector.shape)

def normalize(block):
    group_size = block.shape[-2] * (block.shape[-1] // GROUPS)
    center = grouped(lax.optimization_barrier(jnp.sum(block, axis=-2, keepdims=True))) / group_size
    shifted = block - center
    spread = grouped(lax.optimization_barrier(jnp.sum(shifted * shifted, axis=-2, keepdims=True))) / group_size
    inv_scale = lax.rsqrt(spread + EPSILON)
    return (shifted * inv_scale, inv_scale)

def normalize_back(d_normed, normed, inv_scale):
    group_size = normed.shape[-2] * (normed.shape[-1] // GROUPS)
    mean_first = grouped(lax.optimization_barrier(jnp.sum(d_normed, axis=-2, keepdims=True))) / group_size
    mean_second = grouped(lax.optimization_barrier(jnp.sum(d_normed * normed, axis=-2, keepdims=True))) / group_size
    return inv_scale * (d_normed - mean_first - normed * mean_second)

def matmul(left, weight):
    in_shape = left.shape
    flattened = left.reshape(-1, in_shape[-1])
    product = jnp.dot(flattened, weight, preferred_element_type=jnp.float32)
    return product.reshape(in_shape[:-1] + (weight.shape[1],))

def matmul_transposed(left, weight):
    in_shape = left.shape
    flattened = left.reshape(-1, in_shape[-1])
    product = lax.dot_general(flattened, weight, (((1,), (1,)), ((), ())), preferred_element_type=jnp.float32)
    return product.reshape(in_shape[:-1] + (weight.shape[0],))

def swish_slope(pre_act):
    sigmoid_val = jax.nn.sigmoid(pre_act)
    return sigmoid_val * (1.0 + pre_act * (1.0 - sigmoid_val))

def encode_core(state_in, weight_in, weight_out, weight_skip, condition):
    current = state_in.astype(jnp.float32)
    normed, inv_scale = normalize(current)
    normed_low = normed.astype(jnp.bfloat16)
    pre_act = matmul(normed_low, weight_in) + condition
    hidden = jax.nn.silu(pre_act).astype(jnp.bfloat16)
    result = (current + matmul(hidden, weight_out)).astype(jnp.bfloat16)
    return (current, normed, inv_scale, normed_low, pre_act, hidden, result)

def encode(state_in, weight_in, weight_out, weight_skip, condition):
    parts = encode_core(state_in, weight_in, weight_out, weight_skip, condition)
    result = parts[6]
    skip_out = matmul(result, weight_skip).astype(jnp.bfloat16)
    return (result, skip_out)

def encode_back(state_in, weight_in, weight_out, weight_skip, condition, d_result, d_skip, weight_grad):
    current, normed, inv_scale, normed_low, pre_act, hidden, result = encode_core(state_in, weight_in, weight_out, weight_skip, condition)
    d_total = d_result.astype(jnp.float32) + matmul_transposed(d_skip, weight_skip)
    grad_skip = weight_grad(result, d_skip)
    d_total_low = d_total.astype(jnp.bfloat16)
    grad_out = weight_grad(hidden, d_total_low)
    d_act = (matmul_transposed(d_total_low, weight_out) * swish_slope(pre_act)).astype(jnp.bfloat16)
    grad_in = weight_grad(normed_low, d_act)
    d_normed = matmul_transposed(d_act, weight_in)
    d_inputs = (d_total + normalize_back(d_normed, normed, inv_scale)).astype(jnp.bfloat16)
    return (d_inputs, grad_in, grad_out, grad_skip)

def decode_core(state_in, skip_in, weight_in, weight_out, weight_skip, condition):
    current = state_in.astype(jnp.float32) + matmul(skip_in, weight_skip)
    normed, inv_scale = normalize(current)
    normed_low = normed.astype(jnp.bfloat16)
    pre_act = matmul(normed_low, weight_in) + condition
    hidden = jax.nn.silu(pre_act).astype(jnp.bfloat16)
    return (current, normed, inv_scale, normed_low, pre_act, hidden)

def decode(state_in, skip_in, weight_in, weight_out, weight_skip, condition):
    current, normed, inv_scale, normed_low, pre_act, hidden = decode_core(state_in, skip_in, weight_in, weight_out, weight_skip, condition)
    return (current + matmul(hidden, weight_out)).astype(jnp.bfloat16)

def decode_back(state_in, skip_in, weight_in, weight_out, weight_skip, condition, d_result, weight_grad):
    current, normed, inv_scale, normed_low, pre_act, hidden = decode_core(state_in, skip_in, weight_in, weight_out, weight_skip, condition)
    grad_out = weight_grad(hidden, d_result)
    d_act = (matmul_transposed(d_result, weight_out) * swish_slope(pre_act)).astype(jnp.bfloat16)
    grad_in = weight_grad(normed_low, d_act)
    d_normed = matmul_transposed(d_act, weight_in)
    d_current = (d_result.astype(jnp.float32) + normalize_back(d_normed, normed, inv_scale)).astype(jnp.bfloat16)
    grad_skip = weight_grad(skip_in, d_current)
    d_skip = matmul_transposed(d_current, weight_skip).astype(jnp.bfloat16)
    return (d_current, d_skip, grad_in, grad_out, grad_skip)

def time_embedding(steps, channels):
    half_width = channels // 2
    freqs = jnp.exp(-math.log(10000.0) * jnp.arange(half_width, dtype=jnp.float32) / half_width)
    angles = steps.astype(jnp.float32)[:, None] * freqs[None, :]
    return jnp.concatenate([jnp.cos(angles), jnp.sin(angles)], axis=-1)

def group_grad(left, right):
    left_groups = left.reshape(N_DP, -1, left.shape[-1]).astype(jnp.float32)
    right_groups = right.reshape(N_DP, -1, right.shape[-1]).astype(jnp.float32)
    return jnp.einsum('grc,grd->gcd', left_groups, right_groups, precision=lax.Precision.HIGHEST)

def finish(per_group):
    rounded = per_group.astype(jnp.bfloat16)
    rounded = lax.optimization_barrier(rounded)
    return lax.optimization_barrier(jnp.sum(rounded.astype(jnp.float32), axis=0))

def reference(features, timesteps, text_ids, text_table, in_weights, out_weights, skip_weights, cotangent):
    segments = in_weights.shape[0]
    half_segments = segments // 2
    batch_size = timesteps.shape[0]
    channels = features.shape[-1]
    pooled = lax.optimization_barrier(jnp.mean(jnp.take(text_table, text_ids, axis=0).astype(jnp.float32), axis=1))
    condition = (time_embedding(timesteps, channels) + pooled)[:, None, :]
    current = features.reshape(batch_size, -1, channels)
    inputs = []
    skip_list = []
    for section in range(half_segments):
        inputs.append(current)
        current, skip_out = encode(current, in_weights[section], out_weights[section], skip_weights[section], condition)
        skip_list.append(skip_out)
    for section in range(half_segments, segments):
        inputs.append(current)
        current = decode(current, skip_list[segments - 1 - section], in_weights[section], out_weights[section], skip_weights[section], condition)
    d_current = cotangent.reshape(batch_size, -1, channels)
    grad_in_list = [None] * segments
    grad_out_list = [None] * segments
    grad_skip_list = [None] * segments
    d_skips = [None] * half_segments
    for section in reversed(range(half_segments, segments)):
        d_current, d_skip, grad_in, grad_out, grad_skip = decode_back(inputs[section], skip_list[segments - 1 - section], in_weights[section], out_weights[section], skip_weights[section], condition, d_current, group_grad)
        d_skips[segments - 1 - section] = d_skip
        grad_in_list[section] = finish(grad_in)
        grad_out_list[section] = finish(grad_out)
        grad_skip_list[section] = finish(grad_skip)
    for section in reversed(range(half_segments)):
        d_current, grad_in, grad_out, grad_skip = encode_back(inputs[section], in_weights[section], out_weights[section], skip_weights[section], condition, d_current, d_skips[section], group_grad)
        grad_in_list[section] = finish(grad_in)
        grad_out_list[section] = finish(grad_out)
        grad_skip_list[section] = finish(grad_skip)
    return (jnp.stack(grad_in_list), jnp.stack(grad_out_list), jnp.stack(grad_skip_list))
```

```python
import functools
import math

import jax
import jax.numpy as jnp
from jax import lax
from jax.experimental import pallas as pl
from jax.experimental.pallas import tpu as pltpu
from jax.sharding import PartitionSpec as P

GROUPS = 32
EPSILON = 1e-05
F32 = jnp.float32
BF16 = jnp.bfloat16


def dot(left, right):
    return jnp.dot(left, right, preferred_element_type=F32)


def dot_t(left, right):
    return lax.dot_general(left, right, (((1,), (1,)), ((), ())), preferred_element_type=F32)


def dot_tn(left, right):
    return lax.dot_general(left, right, (((0,), (0,)), ((), ())), preferred_element_type=F32)


def group_sum(rows, members):
    count = rows.shape[0]
    high = rows.astype(BF16)
    rest = rows - high.astype(F32)
    middle = rest.astype(BF16)
    low = (rest - middle.astype(F32)).astype(BF16)
    total = dot(jnp.concatenate([high, middle, low], axis=0), members)
    return total[:count] + total[count : 2 * count] + total[2 * count :]


def pad_rows(rows):
    extra = -rows.shape[0] % 8
    if extra == 0:
        return rows
    return jnp.concatenate([rows, jnp.zeros((extra, rows.shape[1]), F32)], axis=0)


def norm(block, members, count):
    channels = block.shape[-1]
    rows = block.shape[0] // count
    share = 1.0 / (rows * (channels // GROUPS))
    split = block.reshape(count, rows, channels)
    center = group_sum(pad_rows(jnp.sum(split, axis=1)), members) * share
    shifted = split - center[:count][:, None, :]
    spread = group_sum(pad_rows(jnp.sum(shifted * shifted, axis=1)), members) * share
    inv_scale = lax.rsqrt(spread + EPSILON)
    return shifted * inv_scale[:count][:, None, :], center, inv_scale


def norm_back(grad, normed, inv_scale, members, count):
    channels = grad.shape[-1]
    rows = grad.shape[0] // count
    share = 1.0 / (rows * (channels // GROUPS))
    split = grad.reshape(count, rows, channels)
    sums = jnp.concatenate([jnp.sum(split, axis=1), jnp.sum(split * normed, axis=1)], axis=0)
    means = group_sum(pad_rows(sums), members) * share
    first = means[:count][:, None, :]
    second = means[count : 2 * count][:, None, :]
    back = inv_scale[:count][:, None, :] * (split - first - normed * second)
    return back.reshape(grad.shape)


def activate(pre_act):
    sig = jax.nn.sigmoid(pre_act)
    hidden = (pre_act * sig).astype(BF16)
    slope = sig * (1.0 + pre_act * (1.0 - sig))
    return hidden, slope


def block_pre_act(normed_low, weight, cond, count):
    pre_act = dot(normed_low, weight)
    rows = pre_act.shape[0] // count
    return (
        pre_act.reshape(count, rows, -1) + cond[:count][:, None, :]
    ).reshape(pre_act.shape)


def as_low(normed):
    count, rows, channels = normed.shape
    return normed.reshape(count * rows, channels).astype(BF16)


class Loader:
    def __init__(self, core, sems):
        self.core, self.sems, self.used = core, sems, 0

    def pair(self, own, other, slots):
        copies = (
            pltpu.make_async_copy(own, slots.at[self.core], self.sems.at[self.used]),
            pltpu.make_async_copy(other, slots.at[1 - self.core], self.sems.at[self.used + 1]),
        )
        self.used += 2
        for copy in copies:
            copy.start()
        return lambda: [copy.wait() for copy in copies]


def enc_fwd_kernel(
    count, core_ref, x_ref, cond_ref, members_ref, own_in, oth_in, own_out, oth_out,
    x1_ref, x2_ref, hid_ref, low_ref, slope0_ref, slope1_ref, stat_ref, low0_ref,
    w_in, w_out, sems,
):
    core = core_ref[0]
    loader = Loader(core, sems)
    in_ready = loader.pair(own_in, oth_in, w_in)
    out_ready = loader.pair(own_out, oth_out, w_out)
    members = members_ref[...]
    cond = cond_ref[...]

    x0 = x_ref[...].astype(F32)
    normed, center0, scale0 = norm(x0, members, count)
    low0 = as_low(normed)
    in_ready()
    hid0, slope0 = activate(block_pre_act(low0, w_in[0], cond, count))
    slope0_ref[...] = slope0
    out_ready()
    x1 = (x0 + dot(hid0, w_out[0])).astype(BF16)
    x1_ref[...] = x1

    x1 = x1.astype(F32)
    normed, center1, scale1 = norm(x1, members, count)
    low1 = as_low(normed)
    hid1, slope1 = activate(block_pre_act(low1, w_in[1], cond, count))
    slope1_ref[...] = slope1
    x2_ref[...] = (x1 + dot(hid1, w_out[1])).astype(BF16)

    stat_ref[0] = center0
    stat_ref[1] = scale0
    stat_ref[2] = center1
    stat_ref[3] = scale1
    even = core == 0
    hid_ref[...] = jnp.where(even, hid0, hid1)
    low_ref[...] = jnp.where(even, low0, low1)


def dec_kernel(
    count, combine, core_ref, x_ref, m0_ref, m1_ref, cond_ref, d_ref, members_ref,
    own_in, oth_in, own_out, oth_out, own_skip, oth_skip, own_mir, oth_mir,
    down_ref, high_ref, low_back_ref,
    l_out_ref, r_out_ref, l_in_ref, r_in_ref, l_skip_ref, r_skip_ref, l_mir_ref, r_mir_ref,
    w_in, w_out, w_skip, w_mir, sems,
):
    core = core_ref[0]
    loader = Loader(core, sems)
    mir_ready = loader.pair(own_mir, oth_mir, w_mir)
    skip_ready = loader.pair(own_skip, oth_skip, w_skip)
    in_ready = loader.pair(own_in, oth_in, w_in)
    out_ready = loader.pair(own_out, oth_out, w_out)
    members = members_ref[...]
    cond = cond_ref[...]
    m0 = m0_ref[...]
    m1 = m1_ref[...]
    d_in = d_ref[...]

    mir_ready()
    skip_e = dot(m1, w_mir[1]).astype(BF16)
    skip_o = dot(m0, w_mir[0]).astype(BF16)
    skip_ready()
    z_e = x_ref[...].astype(F32) + dot(skip_e, w_skip[0])
    norm_e, _, scale_e = norm(z_e, members, count)
    low_e = as_low(norm_e)
    in_ready()
    hid_e, slope_e = activate(block_pre_act(low_e, w_in[0], cond, count))
    out_ready()
    x_o = (z_e + dot(hid_e, w_out[0])).astype(BF16)

    z_o = x_o.astype(F32) + dot(skip_o, w_skip[1])
    norm_o, _, scale_o = norm(z_o, members, count)
    low_o = as_low(norm_o)
    hid_o, slope_o = activate(block_pre_act(low_o, w_in[1], cond, count))

    e_o = (dot_t(d_in, w_out[1]) * slope_o).astype(BF16)
    back_o = norm_back(dot_t(e_o, w_in[1]), norm_o, scale_o, members, count)
    g_o = (d_in.astype(F32) + back_o).astype(BF16)

    e_e = (dot_t(g_o, w_out[0]) * slope_e).astype(BF16)
    back_e = norm_back(dot_t(e_e, w_in[0]), norm_e, scale_e, members, count)
    g_e = (g_o.astype(F32) + back_e).astype(BF16)

    q_e = dot_t(g_e, w_skip[0]).astype(BF16)
    high = dot_t(q_e, w_mir[1])
    if combine:
        down_ref[...] = (g_e.astype(F32) + high).astype(BF16)
    else:
        down_ref[...] = g_e
        high_ref[...] = high.astype(BF16)
    q_o = dot_t(g_o, w_skip[1]).astype(BF16)
    low_back_ref[...] = dot_t(q_o, w_mir[0]).astype(BF16)

    even = core == 0
    l_out_ref[...] = jnp.where(even, hid_e, hid_o)
    r_out_ref[...] = jnp.where(even, g_o, d_in)
    l_in_ref[...] = jnp.where(even, low_e, low_o)
    r_in_ref[...] = jnp.where(even, e_e, e_o)
    l_skip_ref[...] = jnp.where(even, skip_e, skip_o)
    r_skip_ref[...] = jnp.where(even, g_e, g_o)
    l_mir_ref[...] = jnp.where(even, m0, m1)
    r_mir_ref[...] = jnp.where(even, q_o, q_e)


def enc_back_kernel(
    count, combine, core_ref, d_ref, high_ref, low_back_ref, x0_ref, low0_ref, x1_ref,
    slope0_ref, slope1_ref, stat_ref, members_ref,
    own_in, oth_in, own_out, oth_out,
    down_ref, r_out_ref, r_in_ref,
    w_in, w_out, sems,
):
    core = core_ref[0]
    loader = Loader(core, sems)
    out_ready = loader.pair(own_out, oth_out, w_out)
    in_ready = loader.pair(own_in, oth_in, w_in)
    members = members_ref[...]
    channels = x1_ref.shape[-1]

    t1 = d_ref[...].astype(F32)
    if not combine:
        t1 = t1 + high_ref[...].astype(F32)
    low_t1 = t1.astype(BF16)
    out_ready()
    e1 = (dot_t(low_t1, w_out[1]) * slope1_ref[...]).astype(BF16)
    in_ready()
    x1 = x1_ref[...].astype(F32).reshape(count, -1, channels)
    scale1 = stat_ref[3]
    normed1 = (x1 - stat_ref[2][:count][:, None, :]) * scale1[:count][:, None, :]
    back1 = norm_back(dot_t(e1, w_in[1]), normed1, scale1, members, count)
    d1 = (t1 + back1).astype(BF16)
    t0 = d1.astype(F32) + low_back_ref[...].astype(F32)
    low_t0 = t0.astype(BF16)
    e0 = (dot_t(low_t0, w_out[0]) * slope0_ref[...]).astype(BF16)
    if not combine:
        x0 = x0_ref[...].astype(F32).reshape(count, -1, channels)
        scale0 = stat_ref[1]
        normed0 = (x0 - stat_ref[0][:count][:, None, :]) * scale0[:count][:, None, :]
        back0 = norm_back(dot_t(e0, w_in[0]), normed0, scale0, members, count)
        down_ref[...] = (t0 + back0).astype(BF16)
    even = core == 0
    r_out_ref[...] = jnp.where(even, low_t0, low_t1)
    r_in_ref[...] = jnp.where(even, e0, e1)


def products_kernel(la_ref, ra_ref, lb_ref, rb_ref, a_ref, b_ref):
    a_ref[...] = dot_tn(la_ref[...], ra_ref[...]).astype(BF16)
    b_ref[...] = dot_tn(lb_ref[...], rb_ref[...]).astype(BF16)


VMEM = pl.BlockSpec(memory_space=pltpu.VMEM)
SMEM = pl.BlockSpec(memory_space=pltpu.SMEM)
ANY = pl.BlockSpec(memory_space=pl.ANY)


def pair_scratch(channels, pairs):
    return [pltpu.VMEM((2, channels, channels), BF16) for _ in range(pairs)] + [
        pltpu.SemaphoreType.DMA((2 * pairs,))
    ]


def estimate(rows, channels, products):
    return pl.CostEstimate(
        flops=2 * rows * channels * channels * products,
        bytes_accessed=2 * channels * channels * products,
        transcendentals=0,
    )


def enc_fwd(count, core, x, cond, members, w):
    rows, channels = x.shape
    low = jax.ShapeDtypeStruct((rows, channels), BF16)
    wide = jax.ShapeDtypeStruct((rows, channels), F32)
    stat = jax.ShapeDtypeStruct((4, cond.shape[0], channels), F32)
    tiny = jax.ShapeDtypeStruct((8, 128), BF16)
    return pl.pallas_call(
        functools.partial(enc_fwd_kernel, count),
        out_shape=(low, low, low, low, wide, wide, stat, tiny),
        in_specs=[SMEM] + [VMEM] * 3 + [ANY] * 4,
        out_specs=(VMEM,) * 8,
        scratch_shapes=pair_scratch(channels, 2),
        cost_estimate=estimate(rows, channels, 4),
        name="enc_fwd",
    )(core, x, cond, members, *w["in"], *w["out"])


def dec_both(count, combine, core, x, m0, m1, cond, d, members, w):
    rows, channels = x.shape
    low = jax.ShapeDtypeStruct((rows, channels), BF16)
    tiny = jax.ShapeDtypeStruct((8, 128), BF16)
    return pl.pallas_call(
        functools.partial(dec_kernel, count, combine),
        out_shape=(low, tiny if combine else low) + (low,) * 9,
        in_specs=[SMEM] + [VMEM] * 6 + [ANY] * 8,
        out_specs=(VMEM,) * 11,
        scratch_shapes=pair_scratch(channels, 4),
        cost_estimate=estimate(rows, channels, 15),
        name="dec_both",
    )(core, x, m0, m1, cond, d, members, *w["in"], *w["out"], *w["skip"], *w["mirror"])


def enc_back(count, combine, core, d, high, low_back, x0, x1, slopes, stat, members, w):
    rows, channels = x1.shape
    low = jax.ShapeDtypeStruct((rows, channels), BF16)
    tiny = jax.ShapeDtypeStruct((8, 128), BF16)
    return pl.pallas_call(
        functools.partial(enc_back_kernel, count, combine),
        out_shape=(tiny if combine else low, low, low),
        in_specs=[SMEM] + [VMEM] * 10 + [ANY] * 4,
        out_specs=(VMEM,) * 3,
        scratch_shapes=pair_scratch(channels, 2),
        cost_estimate=estimate(rows, channels, 4),
        name="enc_back",
    )(core, d, high, low_back, x0, x0, x1, *slopes, stat, members, *w["in"], *w["out"])


def products(la, ra, lb, rb):
    rows, channels = la.shape
    out = jax.ShapeDtypeStruct((channels, channels), BF16)
    return pl.pallas_call(
        products_kernel,
        out_shape=(out, out),
        in_specs=[VMEM] * 4,
        out_specs=(VMEM,) * 2,
        cost_estimate=estimate(rows, channels, 2),
        name="products",
    )(la, ra, lb, rb)


def swap_core(block):
    count = lax.axis_size("segment")
    return lax.ppermute(block, "segment", [(s, s ^ 1) for s in range(count)])


def mirror_chip(block):
    count = lax.axis_size("segment")
    chips = count // 2
    route = [(s, 2 * (chips - 1 - s // 2) + s % 2) for s in range(count)]
    return lax.ppermute(block, "segment", [pair for pair in route if pair[0] != pair[1]])


def next_chip(block, steps):
    count = lax.axis_size("segment")
    route = [(s, s + 2 * steps) for s in range(count) if 0 <= s + 2 * steps < count]
    return lax.ppermute(block, "segment", route)


def factors_of(size):
    found, rest, stride = [], size, 1
    while rest > 1:
        step = next(k for k in range(2, rest + 1) if rest % k == 0)
        found.append((stride, step))
        stride *= step
        rest //= step
    return found


def exchange(block, axis, stride, step, name):
    size = lax.axis_size(name)
    place = lax.axis_index(name) // stride % step
    total = lax.dynamic_index_in_dim(block, place, axis, keepdims=False).astype(F32)
    for offset in range(1, step):
        route = []
        for d in range(size):
            p = d // stride % step
            route.append((d, d + (((p + offset) % step) - p) * stride))
        sent = lax.dynamic_index_in_dim(block, (place + offset) % step, axis, keepdims=False)
        total = total + lax.ppermute(sent, name, route).astype(F32)
    return total


def halving(block, order, name):
    size = lax.axis_size(name)
    factors = factors_of(size)
    dims = [step for _, step in reversed(factors)]
    total = block.reshape(dims + [block.shape[0] // size] + list(block.shape[1:]))
    left = list(reversed(range(len(factors))))
    for which in order:
        stride, step = factors[which]
        axis = left.index(which)
        total = exchange(total.astype(block.dtype), axis, stride, step, name)
        left.remove(which)
    return total


def orders_of(size):
    count = len(factors_of(size))
    first = list(range(count))
    return first, first[1:] + first[:1]


def scatter_pair(first, second, name):
    order_a, order_b = orders_of(lax.axis_size(name))
    return halving(first, order_a, name), halving(second, order_b, name)


def time_embedding(steps, channels):
    half_width = channels // 2
    freqs = jnp.exp(-math.log(10000.0) * jnp.arange(half_width, dtype=F32) / half_width)
    angles = steps.astype(F32)[:, None] * freqs[None, :]
    return jnp.concatenate([jnp.cos(angles), jnp.sin(angles)], axis=-1)


def pooled_text(text_ids, text_table, micro_count):
    vocab_rows = text_table.shape[0]
    first_word = lax.axis_index(("dp", "segment")) * vocab_rows
    vocab_ids = first_word + lax.iota(jnp.int32, vocab_rows)
    counts = jnp.sum((text_ids[None, :, :] == vocab_ids[:, None, None]).astype(F32), axis=-1)
    partial = lax.dot_general(
        counts.astype(BF16), text_table, (((0,), (0,)), ((), ())), preferred_element_type=F32
    )
    partial = partial + swap_core(partial)
    size = lax.axis_size("dp")
    total = halving(partial, orders_of(size)[0], "dp")
    count = lax.axis_size("segment")
    stride = 2
    for _, step in factors_of(count // 2):
        part = total
        for offset in range(1, step):
            route = []
            for s in range(count):
                p = s // stride % step
                route.append((s, s + (((p + offset) % step) - p) * stride))
            total = total + lax.ppermute(part, "segment", route)
        stride *= step
    return total / text_ids.shape[1]


def keep(active, new, old):
    if old is None:
        return new
    return jax.tree.map(lambda n, o: jnp.where(active, n, o), new, old)


def dec_forward(count, x, m0, m1, cond, members, even, w):
    def sorted_pair(pair):
        own, other = pair
        return jnp.where(even, own, other), jnp.where(even, other, own)

    w_in, w_out, w_skip, w_mir = (sorted_pair(w[k]) for k in ("in", "out", "skip", "mirror"))
    for slot, source in ((0, m1), (1, m0)):
        skip = dot(source, w_mir[1 - slot]).astype(BF16)
        z = x.astype(F32) + dot(skip, w_skip[slot])
        low = as_low(norm(z, members, count)[0])
        hidden, _ = activate(block_pre_act(low, w_in[slot], cond, count))
        x = (z + dot(hidden, w_out[slot])).astype(BF16)
    return x


def on_device(
    features, timesteps, text_ids, text_table, in_weights, out_weights, skip_weights, cotangent
):
    segments = lax.axis_size("segment")
    chips = segments // 2
    half = chips // 2
    segment = lax.axis_index("segment")
    chip = segment // 2
    core = (segment % 2).astype(jnp.int32).reshape(1)
    is_dec = chip >= half
    channels = features.shape[-1]
    count = timesteps.shape[0]
    single = half == 1

    own_in, own_out, own_skip = in_weights[0], out_weights[0], skip_weights[0]
    own_mirror = mirror_chip(own_skip)
    w = {
        "in": (own_in, swap_core(own_in)),
        "out": (own_out, swap_core(own_out)),
        "skip": (own_skip, swap_core(own_skip)),
        "mirror": (own_mirror, swap_core(own_mirror)),
    }
    group = lax.iota(jnp.int32, channels) // (channels // GROUPS)
    members = (group[:, None] == group[None, :]).astype(BF16)

    cond = time_embedding(timesteps, channels) + pooled_text(text_ids, text_table, count)
    cond = jnp.pad(cond, ((0, -count % 8), (0, 0)))

    state, saved = features, None
    for j in range(half):
        x1, x2, hidden, low, slope0, slope1, stat, _ = enc_fwd(
            count, core, state, cond, members, w
        )
        saved = keep(chip == j, (state, x1, x2, hidden, low, slope0, slope1, stat), saved)
        if not single:
            state = next_chip(x2, 1)
    x0, x1, x2, enc_hidden, enc_low, slope0, slope1, stat = saved
    m0, m1 = mirror_chip(x1), mirror_chip(x2)
    if single:
        state = m1

    entry = None
    for j in range(half):
        entry = keep(chip == half + j, state, entry)
        if j < half - 1:
            state = next_chip(
                dec_forward(count, state, m0, m1, cond, members, core[0] == 0, w), 1
            )

    d_in, saved = cotangent, None
    for j in reversed(range(half)):
        outs = dec_both(count, single, core, entry, m0, m1, cond, d_in, members, w)
        saved = keep(chip == half + j, outs, saved)
        d_in = next_chip(outs[0], -1) if not single else mirror_chip(outs[0])
    _, high, low_back, l_out, r_out, l_in, r_in, l_skip, r_skip, l_mir, r_mir = saved
    low_back = mirror_chip(low_back)
    if not single:
        high = mirror_chip(high)
    skip_pair = products(l_skip, r_skip, l_mir, r_mir)
    own_skip_grad, mirror_skip_grad = scatter_pair(*skip_pair, "dp")
    mirror_skip_grad = mirror_chip(mirror_skip_grad)

    saved = None
    for j in reversed(range(half)):
        outs = enc_back(
            count, single, core, d_in, high, low_back, x0, x1, (slope0, slope1), stat, members, w
        )
        saved = keep(chip == j, outs, saved)
        if not single and j > 0:
            d_in = next_chip(outs[0], -1)
    _, enc_r_out, enc_r_in = saved

    pair = products(
        jnp.where(is_dec, l_out, enc_hidden),
        jnp.where(is_dec, r_out, enc_r_out),
        jnp.where(is_dec, l_in, enc_low),
        jnp.where(is_dec, r_in, enc_r_in),
    )
    grad_out, grad_in = scatter_pair(*pair, "dp")
    grad_skip = jnp.where(is_dec, own_skip_grad, mirror_skip_grad)
    return (grad_in[None], grad_out[None], grad_skip[None])


def solution(mesh):
    in_specs = (
        P("dp", None),
        P("dp"),
        P(),
        P(("dp", "segment"), None),
        P("segment", None, None),
        P("segment", None, None),
        P("segment", None, None),
        P("dp", None),
    )
    out_specs = (P("segment", "dp", None), P("segment", "dp", None), P("segment", "dp", None))
    return jax.shard_map(
        on_device, mesh=mesh, in_specs=in_specs, out_specs=out_specs, check_vma=False
    )
```
